256 devices in a mesh: ctx: 64 (over y, z, core), head: 4 (over x).
Axes of the slice: x: 4, y: 4, z: 8, core: 2. Of those that a mesh axis runs over, the one named last changes fastest.
Arguments:
- query: bfloat16 [64, 2, 512, 4096], P('ctx', None, None, 'head'), may hold values from -48 to 48
- key: bfloat16 [64, 2, 512, 512], P('ctx', None, 'head'), may hold values from -18 to 18
- value: bfloat16 [64, 2, 512, 512], P('ctx', None, 'head'), may hold values from -6 to 6
- d_out: bfloat16 [64, 2, 512, 4096], P('ctx', None, None, 'head'), may hold values from -6 to 6
- doc_start: int32 [512], replicated, may hold values from 0 to 1, as said below
Outputs:
- d_query: bfloat16 [64, 2, 512, 4096], P('ctx', None, None, 'head')
- d_key: bfloat16 [64, 2, 512, 512], P('ctx', None, 'head')
- d_value: bfloat16 [64, 2, 512, 512], P('ctx', None, 'head')
The draws below stay inside these ranges and needn't reach their ends.
Inputs may be any that keep to these rules, and one draw needn't show every extreme that they name: `doc_start`: 1 where a document begins at that block of 128 tokens (blocks in sequence order); block 0 begins one; from every beginning the next beginning, or the end of the sequence, is 1 to 3 blocks away; the first block of every span after the first lies inside a document of exactly 3 blocks that began in the span before.
All inputs are finite; a program needn't handle non-finite values.
Results may differ from the reference program's by a relative error of at most 0.039.
Values may be sent and summed in bfloat16 or wider, within the bound.
A program may use at most 64 MiB of HBM per device.

```python
import jax
import jax.numpy as jnp
from jax import lax

QH = 32
KVH = 4
HD = 128
BLK = 128
LMAX_BLK = 3
GROUP = 8
CH = 512
CHB = 4
NCHUNK = 128
S_BLK = 512
TAIL = 256
N_CTX = 64


def key_parts(key):
    common = jax.random.fold_in(key, 21)
    drawn = jax.random.truncated_normal(jax.random.fold_in(common, 3), -6.0, 6.0, (NCHUNK // 2, 2, CH, KVH * HD), jnp.float32)
    return drawn


def draw_key(key, part):
    drawn = key_parts(key)
    return drawn.astype(jnp.bfloat16)


def draw_query(key, part):
    own_key = jax.random.fold_in(key, 31)
    drawn_query = jax.random.truncated_normal(jax.random.fold_in(own_key, 4), -6.0, 6.0, (NCHUNK // 2, 2, CH, QH * HD), jnp.float32)
    return drawn_query.astype(jnp.bfloat16)


def draw_doc_start(key, part):
    gaps = jax.random.randint(jax.random.fold_in(key, 11), (S_BLK,), 1, LMAX_BLK + 1)
    beginnings = jnp.cumsum(gaps) - gaps
    positions = jnp.arange(S_BLK, dtype=jnp.int32)
    flags = jnp.any(beginnings[None, :] == positions[:, None], axis=1)
    span_ids = jnp.arange(1, NCHUNK, dtype=jnp.int32)
    backward = jax.random.randint(jax.random.fold_in(key, 13), (NCHUNK - 1,), 1, LMAX_BLK)
    openings = span_ids * CHB - backward
    closings = openings + LMAX_BLK
    inside = jnp.any((positions[:, None] > openings[None, :]) & (positions[:, None] < closings[None, :]), axis=1)
    endpoint = jnp.any((positions[:, None] == openings[None, :]) | (positions[:, None] == closings[None, :]), axis=1)
    flags = jnp.where(inside, False, flags)
    flags = jnp.where(endpoint, True, flags)
    return flags.astype(jnp.int32)


def steps_of(key, dims, split, low, largest):
    loudness, own = 1.0, jax.random.fold_in(key, 6)
    for axis_at, shards_of in split:
        heights = jnp.exp(jax.random.uniform(jax.random.fold_in(own, axis_at), (shards_of,), jnp.float32, low / len(split), largest / len(split)))
        loudness = loudness * jnp.repeat(heights, dims[axis_at] // shards_of).reshape([-1 if axis == axis_at else 1 for axis in range(len(dims))])
    return loudness


def noise(rng, extent, deviation, bound, cuts=(), held_as=jnp.bfloat16):
    factor_of = steps_of(rng, extent, cuts, -0.22, 0.18) if cuts else 1.0
    drawn = jax.random.normal(rng, extent, jnp.float32) * deviation * factor_of
    return jnp.minimum(jnp.maximum(drawn, -bound), bound).astype(held_as)


def setup_inputs(seed: int = 0) -> dict:
    streams_of = jax.random.split(jax.random.key(seed), 6)
    return {
        "query": draw_query(jax.random.fold_in(streams_of[5], 71), 0),
        "key": draw_key(jax.random.fold_in(streams_of[5], 71), 0),
        "value": noise(streams_of[2], (N_CTX, 2, CH, KVH * HD), 1.0, 6.0, ((0, 64), (2, 4))),
        "d_out": noise(streams_of[3], (N_CTX, 2, CH, QH * HD), 1.0, 6.0, ((0, 64), (3, 4))),
        "doc_start": draw_doc_start(jax.random.fold_in(streams_of[5], 71), 0),
    }


def unfolded(array):
    return jnp.concatenate([array[:, 0], array[::-1, 1]], axis=0)


def refolded(array):
    halves = array.shape[0] // 2
    return jnp.stack([array[:halves], array[halves:][::-1]], axis=1)


def rounded(values):
    return lax.optimization_barrier(values.astype(jnp.bfloat16)).astype(jnp.float32)


def windowed(extended):
    pieces = []
    for offset in range(LMAX_BLK):
        sliced = lax.slice_in_dim(extended, offset * BLK, offset * BLK + CH, axis=0)
        pieces.append(sliced.reshape((CHB, BLK) + extended.shape[1:]))
    return jnp.concatenate(pieces, axis=1)


def unwindowed(windows):
    summed = jnp.zeros((TAIL + CH,) + windows.shape[2:], jnp.float32)
    for offset in range(LMAX_BLK):
        sliced = windows[:, offset * BLK:(offset + 1) * BLK].reshape((CH,) + windows.shape[2:])
        summed = summed.at[offset * BLK:offset * BLK + CH].add(sliced)
    return summed


def span_terms(operands):
    queries, grads_out, keys_ext, values_ext, doc_begins, span_start = operands
    score_scale = HD ** -0.5
    q_blocks = queries.reshape(CHB, BLK, KVH, GROUP, HD).astype(jnp.float32)
    do_blocks = grads_out.reshape(CHB, BLK, KVH, GROUP, HD).astype(jnp.float32)
    k_windows = windowed(keys_ext).astype(jnp.float32)
    v_windows = windowed(values_ext).astype(jnp.float32)
    row_pos = jnp.arange(BLK, dtype=jnp.int32)[None, :, None]
    col_pos = jnp.arange(LMAX_BLK * BLK, dtype=jnp.int32)[None, None, :]
    key_pos = span_start - TAIL + jnp.arange(CHB, dtype=jnp.int32)[:, None, None] * BLK + col_pos
    visible = (col_pos <= row_pos + TAIL) & (key_pos >= doc_begins[:, None, None])
    visible = visible[:, None, None]
    scores = jnp.einsum('btgjd,bkgd->bgjtk', q_blocks, k_windows) * score_scale
    peak = jnp.max(jnp.where(visible, scores, -1e30), axis=-1, keepdims=True)
    weights = jnp.exp(jnp.where(visible, scores - peak, -1e30))
    probs = weights / jnp.sum(weights, axis=-1, keepdims=True)
    probs_b = rounded(probs)
    outputs = rounded(jnp.einsum('bgjtk,bkgd->btgjd', probs_b, v_windows))
    deltas = jnp.sum(do_blocks * outputs, axis=-1)
    dprobs = jnp.einsum('btgjd,bkgd->bgjtk', do_blocks, v_windows)
    dscores = rounded(probs * (dprobs - jnp.transpose(deltas, (0, 2, 3, 1))[..., None]) * score_scale)
    d_queries = jnp.einsum('bgjtk,bkgd->btgjd', dscores, k_windows).astype(jnp.bfloat16)
    dk_windows = jnp.einsum('bgjtk,btgjd->bkgd', dscores, q_blocks)
    dv_windows = jnp.einsum('bgjtk,btgjd->bkgd', probs_b, do_blocks)
    return (d_queries.reshape(CH, QH * HD),
            unwindowed(dk_windows).reshape(TAIL + CH, KVH * HD),
            unwindowed(dv_windows).reshape(TAIL + CH, KVH * HD))


def extended_lines(array):
    line = unfolded(array).reshape(NCHUNK, CH, KVH, HD)
    leading = jnp.concatenate([jnp.zeros((1, TAIL, KVH, HD), array.dtype), line[:-1, CH - TAIL:]], axis=0)
    return jnp.concatenate([leading, line], axis=1)


def reference(query, key, value, d_out, doc_start):
    line_q = unfolded(query)
    line_do = unfolded(d_out)
    ext_k = extended_lines(key)
    ext_v = extended_lines(value)
    run_begin = lax.cummax(jnp.where(doc_start == 1, jnp.arange(S_BLK, dtype=jnp.int32), 0), axis=0) * BLK
    begins = run_begin.reshape(NCHUNK, CHB)
    starts = jnp.arange(NCHUNK, dtype=jnp.int32) * CH
    line_dq, dk_ext, dv_ext = lax.map(span_terms, (line_q, line_do, ext_k, ext_v, begins, starts))
    dk_line = dk_ext[:, TAIL:].at[:-1, CH - TAIL:].add(dk_ext[1:, :TAIL])
    dv_line = dv_ext[:, TAIL:].at[:-1, CH - TAIL:].add(dv_ext[1:, :TAIL])
    d_query = refolded(line_dq)
    d_key = refolded(dk_line.astype(jnp.bfloat16))
    d_value = refolded(dv_line.astype(jnp.bfloat16))
    return d_query, d_key, d_value
```

```python
import functools

import jax
import jax.numpy as jnp
from jax import lax
from jax.experimental import pallas as pl
from jax.experimental.pallas import tpu as pltpu
from jax.sharding import PartitionSpec as P

F32 = jnp.float32
BF16 = jnp.bfloat16
HD = 128
BLK = 128
HEADS = 8
SPAN = 512
TAIL = 256
EXT = TAIL + SPAN
SCALE = HD**-0.5
SCALE_LOG2E = SCALE * 1.4426950408889634
BIG = 1e30
NT = (((1,), (1,)), ((), ()))
NN = (((1,), (0,)), ((), ()))
MESH = pl.DeviceIdType.MESH


def dot(a, b, dims=NN):
    return lax.dot_general(a, b, dims, preferred_element_type=F32)


def at_block(index):
    if isinstance(index, int):
        return index * BLK
    return pl.multiple_of(index * BLK, BLK)


def block_grads(q_v, do_v, dq_v, kv, acc, docs, tri, slot, span, qb, k0, nk):
    rows = pl.ds(at_block(qb), BLK)
    krows = pl.ds(at_block(k0), nk * BLK)
    kw = kv[0, slot, krows, :]
    vw = kv[1, slot, krows, :]
    g = span * 4 + qb
    hidden = docs[g]
    hide = [hidden]
    for back in range(1, nk - 1):
        hidden = hidden + docs[jnp.maximum(g - back, 0)]
        hide.append(hidden)
    subs = [jnp.where(x > 0, BIG, 0.0).astype(F32) for x in hide][::-1]
    qq = q_v[slot, rows, :]
    dd = do_v[slot, rows, :]
    q2 = jnp.concatenate([qq[:, h * HD : (h + 1) * HD] for h in range(HEADS)], axis=0)
    d2 = jnp.concatenate([dd[:, h * HD : (h + 1) * HD] for h in range(HEADS)], axis=0)
    scores = dot(kw, q2, NT)
    dprobs = dot(vw, d2, NT)
    parts = [scores[i * BLK : (i + 1) * BLK] for i in range(nk)]
    parts[-1] = parts[-1] + tri
    tops = [jnp.max(x, axis=0, keepdims=True) for x in parts]
    top = tops[-1]
    for i in range(nk - 1):
        top = jnp.maximum(top, tops[i] - subs[i])
    top = top * SCALE_LOG2E
    weights = []
    for i in range(nk):
        low = top if i == nk - 1 else top + subs[i]
        weights.append(jnp.exp2(parts[i] * SCALE_LOG2E - low))
    total = sum(jnp.sum(x, axis=0, keepdims=True) for x in weights)
    inverse = 1.0 / total
    probs = jnp.concatenate([x * inverse for x in weights], axis=0)
    probs_b = probs.astype(BF16)
    weighted = probs * dprobs
    delta = jnp.sum(weighted, axis=0, keepdims=True)
    dscores = (weighted - probs * delta).astype(BF16)
    acc[1, slot, krows, :] += dot(probs_b, d2)
    acc[0, slot, krows, :] += dot(dscores, q2)
    dqt = dot(kw.T, dscores) * SCALE
    for h in range(HEADS):
        dq_v[slot, rows, h * HD : (h + 1) * HD] = dqt[:, h * HD : (h + 1) * HD].T.astype(BF16)


def kernel(
    n_ctx,
    n_head,
    q_hbm,
    do_hbm,
    k_hbm,
    v_hbm,
    doc_hbm,
    dq_hbm,
    dkv_hbm,
    q_v,
    do_v,
    dq_v,
    kv,
    acc,
    out_v,
    tail_out,
    tail_in,
    docs,
    load_sem,
    doc_sem,
    store_sem,
    kv_send,
    kv_recv,
    relay_send,
    relay_recv,
    tail_send,
    tail_recv,
    out_send,
    out_recv,
):
    c = lax.axis_index("ctx")
    x = lax.axis_index("head")
    after = lax.rem(c + 1, n_ctx)
    before = lax.rem(c + n_ctx - 1, n_ctx)
    is_first = c == 0
    is_last = c == n_ctx - 1
    first = jnp.where(is_first, 1, 0)

    barrier = pltpu.get_barrier_semaphore()
    for d in range(1, n_head):
        pl.semaphore_signal(
            barrier, inc=1, device_id=(c, lax.rem(x + d, n_head)), device_id_type=MESH
        )
    for other in (after, before):
        pl.semaphore_signal(barrier, inc=1, device_id=(other, x), device_id_type=MESH)

    doc_copy = pltpu.make_async_copy(doc_hbm, docs, doc_sem)
    doc_copy.start()
    sources = (k_hbm, v_hbm)

    def kv_place(which, slot, block):
        return kv.at[which, slot, pl.ds(at_block(block + 2), BLK), :]

    own = []
    for slot in range(2):
        for which in range(2):
            own.append(
                pltpu.make_async_copy(
                    sources[which].at[slot, :, pl.ds(at_block(x), HD)],
                    kv_place(which, slot, x),
                    kv_recv.at[which, slot, x],
                )
            )
            own[-1].start()
    loads = []
    for slot in range(2):
        for i, (src, dst) in enumerate(((q_hbm, q_v), (do_hbm, do_v))):
            loads.append(
                pltpu.make_async_copy(src.at[slot], dst.at[slot], load_sem.at[i, slot])
            )
            loads[-1].start()
    acc[...] = jnp.zeros_like(acc)
    kk = lax.broadcasted_iota(jnp.int32, (BLK, HEADS * BLK), 0)
    qq = lax.broadcasted_iota(jnp.int32, (BLK, HEADS * BLK), 1) % BLK
    tri = jnp.where(kk <= qq, 0.0, -BIG).astype(F32)

    pl.semaphore_wait(barrier, n_head + 1)

    sends = []
    for slot in range(2):
        for which in range(2):
            for d in (2, 1, 3):
                to = lax.rem(x + d, n_head)
                copy = pltpu.make_async_remote_copy(
                    src_ref=sources[which].at[slot, :, pl.ds(at_block(to), HD)],
                    dst_ref=kv_place(which, slot, x),
                    send_sem=kv_send.at[which, slot, d],
                    recv_sem=kv_recv.at[which, slot, x],
                    device_id=(c, to),
                    device_id_type=MESH,
                )
                copy.start()
                sends.append(copy)

    def wait_block(slot, block):
        for which in range(2):
            place = kv_place(which, slot, block)
            pltpu.make_async_copy(place, place, kv_recv.at[which, slot, block]).wait()

    def relay(slot):
        return pltpu.make_async_remote_copy(
            src_ref=kv.at[:, slot, pl.ds(SPAN, TAIL), :],
            dst_ref=kv.at[:, slot, pl.ds(0, TAIL), :],
            send_sem=relay_send.at[slot],
            recv_sem=relay_recv.at[slot],
            device_id=(after if slot == 0 else before, x),
            device_id_type=MESH,
        )

    def send_tail(slot):
        tail_out[slot, 0] = (acc[0, slot, 0:TAIL, :] * SCALE).astype(BF16)
        tail_out[slot, 1] = acc[1, slot, 0:TAIL, :].astype(BF16)
        copy = pltpu.make_async_remote_copy(
            src_ref=tail_out.at[slot],
            dst_ref=tail_in.at[slot],
            send_sem=tail_send.at[slot],
            recv_sem=tail_recv.at[slot],
            device_id=(before if slot == 0 else after, x),
            device_id_type=MESH,
        )
        copy.start()
        return copy

    def out_copies(slot, block):
        place = dkv_hbm.at[:, slot, :, pl.ds(at_block(x), HD)]
        remote = pltpu.make_async_remote_copy(
            src_ref=out_v.at[slot, block],
            dst_ref=place,
            send_sem=out_send.at[slot, block],
            recv_sem=out_recv.at[slot, x],
            device_id=(c, block),
            device_id_type=MESH,
        )
        local = pltpu.make_async_copy(out_v.at[slot, block], place, out_recv.at[slot, x])
        return remote, local

    def send_out(slot, block, extra=None):
        rows = pl.ds((block + 2) * BLK, BLK)
        for which in range(2):
            value = acc[which, slot, rows, :]
            if which == 0:
                value = value * SCALE
            if extra is not None:
                value = value + extra(which, block - 2)
            out_v[slot, block, which] = value.astype(BF16)
        remote, local = out_copies(slot, block)

        @pl.when(x != block)
        def _():
            remote.start()

        @pl.when(x == block)
        def _():
            local.start()

    spans = (c, 2 * n_ctx - 1 - c)
    tools = (q_v, do_v, dq_v, kv, acc, docs, tri)

    wait_block(0, 2)
    wait_block(0, 3)
    relays = [relay(0), relay(1)]
    relays[0].start()
    wait_block(0, 0)
    wait_block(0, 1)
    doc_copy.wait()
    loads[0].wait()
    loads[1].wait()
    block_grads(*tools, 0, spans[0], 3, 4, 2)
    block_grads(*tools, 0, spans[0], 2 - first, 3 - first, 2)
    for block in (2, 3, 0, 1):
        wait_block(1, block)
    relays[1].start()
    relays[0].wait_recv()
    block_grads(*tools, 0, spans[0], 0, 0, 3)
    block_grads(*tools, 0, spans[0], 1 + first, 1 + first, 3)
    tails = [send_tail(0)]
    send_out(0, 0)
    send_out(0, 1)
    stores = [pltpu.make_async_copy(dq_v.at[0], dq_hbm.at[0], store_sem.at[0])]
    stores[0].start()

    loads[2].wait()
    loads[3].wait()
    relays[1].wait_recv()

    @pl.when(is_last)
    def _():
        kv[:, 1, 0:TAIL, :] = kv[:, 0, SPAN : SPAN + TAIL, :]

    def store_rows(block):
        rows = pl.ds(block * BLK, BLK)
        stores.append(
            pltpu.make_async_copy(
                dq_v.at[1, rows, :], dq_hbm.at[1, rows, :], store_sem.at[1 + block]
            )
        )
        stores[-1].start()

    block_grads(*tools, 1, spans[1], 0, 0, 3)
    store_rows(0)
    block_grads(*tools, 1, spans[1], 1, 1, 3)
    store_rows(1)
    tails.append(send_tail(1))
    send_out(1, 0)
    block_grads(*tools, 1, spans[1], 2, 3, 2)
    store_rows(2)
    send_out(1, 1)
    tails[0].wait_recv()

    def extra_first(which, i):
        arrived = tail_in[0, which, i * BLK : (i + 1) * BLK, :].astype(F32)
        mine = tail_out[1, which, i * BLK : (i + 1) * BLK, :].astype(F32)
        return jnp.where(is_last, mine, arrived)

    def extra_second(which, i):
        arrived = tail_in[1, which, i * BLK : (i + 1) * BLK, :].astype(F32)
        return jnp.where(is_first, 0.0, arrived)

    send_out(0, 2, extra_first)
    send_out(0, 3, extra_first)
    block_grads(*tools, 1, spans[1], 3, 3, 3)
    store_rows(3)
    tails[1].wait_recv()
    send_out(1, 2, extra_second)
    send_out(1, 3, extra_second)

    for copy in sends + relays + tails:
        copy.wait_send()
    for slot in range(2):
        for block in range(4):
            remote, _ = out_copies(slot, block)

            @pl.when(x != block)
            def _():
                remote.wait_send()

            place = dkv_hbm.at[:, slot, :, pl.ds(block * HD, HD)]
            pltpu.make_async_copy(place, place, out_recv.at[slot, block]).wait()
    for copy in stores:
        copy.wait()


def per_device(n_ctx, n_head, query, key, value, d_out, doc_start):
    anywhere = pl.BlockSpec(memory_space=pl.ANY)
    dma = pltpu.SemaphoreType.DMA
    dq, dkv = pl.pallas_call(
        functools.partial(kernel, n_ctx, n_head),
        out_shape=(
            jax.ShapeDtypeStruct((2, SPAN, HEADS * HD), BF16),
            jax.ShapeDtypeStruct((2, 2, BLK, n_head * HD), BF16),
        ),
        in_specs=[anywhere] * 5,
        out_specs=(anywhere, anywhere),
        scratch_shapes=[
            pltpu.VMEM((2, SPAN, HEADS * HD), BF16),
            pltpu.VMEM((2, SPAN, HEADS * HD), BF16),
            pltpu.VMEM((2, SPAN, HEADS * HD), BF16),
            pltpu.VMEM((2, 2, EXT, HD), BF16),
            pltpu.VMEM((2, 2, EXT, HD), F32),
            pltpu.VMEM((2, 4, 2, BLK, HD), BF16),
            pltpu.VMEM((2, 2, TAIL, HD), BF16),
            pltpu.VMEM((2, 2, TAIL, HD), BF16),
            pltpu.SMEM(doc_start.shape, jnp.int32),
            dma((2, 2)),
            dma,
            dma((5,)),
            dma((2, 2, 4)),
            dma((2, 2, 4)),
            dma((2,)),
            dma((2,)),
            dma((2,)),
            dma((2,)),
            dma((2, 4)),
            dma((2, 4)),
        ],
        compiler_params=pltpu.CompilerParams(
            collective_id=0, has_side_effects=True, vmem_limit_bytes=56 << 20
        ),
    )(query[0], d_out[0], key[0], value[0], doc_start)
    return dq[None], dkv[0][None], dkv[1][None]


def solution(mesh):
    return jax.shard_map(
        functools.partial(per_device, mesh.shape["ctx"], mesh.shape["head"]),
        mesh=mesh,
        in_specs=(
            P("ctx", None, None, "head"),
            P("ctx", None, "head", None),
            P("ctx", None, "head", None),
            P("ctx", None, None, "head"),
            P(),
        ),
        out_specs=(
            P("ctx", None, None, "head"),
            P("ctx", None, "head", None),
            P("ctx", None, "head", None),
        ),
        check_vma=False,
    )
```

```python
import functools

import jax
import jax.numpy as jnp
from jax import lax
from jax.experimental import pallas as pl
from jax.experimental.pallas import tpu as pltpu
from jax.sharding import PartitionSpec as P

F32 = jnp.float32
BF16 = jnp.bfloat16
HD = 128
BLK = 128
HEADS = 8
SPAN = 512
TAIL = 256
ROW = 16
EXT = TAIL + SPAN
SCALE = HD**-0.5
SCALE_LOG2E = SCALE * 1.4426950408889634
BIG = 1e30
NT = (((1,), (1,)), ((), ()))
NN = (((1,), (0,)), ((), ()))
MESH = pl.DeviceIdType.MESH


def dot(a, b, dims=NN):
    return lax.dot_general(a, b, dims, preferred_element_type=F32)


def at_block(index):
    if isinstance(index, int):
        return index * BLK
    return pl.multiple_of(index * BLK, BLK)


def block_grads(q_v, do_v, dq_v, kv, acc, docs, tri, slot, span, qb, k0, nk):
    rows = pl.ds(at_block(qb), BLK)
    krows = pl.ds(at_block(k0), nk * BLK)
    kw = kv[0, slot, krows, :]
    vw = kv[1, slot, krows, :]
    g = span * 4 + qb
    hidden = docs[g]
    hide = [hidden]
    for back in range(1, nk - 1):
        hidden = hidden + docs[jnp.maximum(g - back, 0)]
        hide.append(hidden)
    subs = [jnp.where(x > 0, BIG, 0.0).astype(F32) for x in hide][::-1]
    qq = q_v[slot, rows, :]
    dd = do_v[slot, rows, :]
    q2 = jnp.concatenate([qq[:, h * HD : (h + 1) * HD] for h in range(HEADS)], axis=0)
    d2 = jnp.concatenate([dd[:, h * HD : (h + 1) * HD] for h in range(HEADS)], axis=0)
    scores = dot(kw, q2, NT)
    dprobs = dot(vw, d2, NT)
    parts = [scores[i * BLK : (i + 1) * BLK] for i in range(nk)]
    parts[-1] = parts[-1] + tri
    tops = [jnp.max(x, axis=0, keepdims=True) for x in parts]
    top = tops[-1]
    for i in range(nk - 1):
        top = jnp.maximum(top, tops[i] - subs[i])
    top = top * SCALE_LOG2E
    weights = []
    for i in range(nk):
        low = top if i == nk - 1 else top + subs[i]
        weights.append(jnp.exp2(parts[i] * SCALE_LOG2E - low))
    total = sum(jnp.sum(x, axis=0, keepdims=True) for x in weights)
    inverse = 1.0 / total
    probs = jnp.concatenate([x * inverse for x in weights], axis=0)
    probs_b = probs.astype(BF16)
    weighted = probs * dprobs
    delta = jnp.sum(weighted, axis=0, keepdims=True)
    dscores = (weighted - probs * delta).astype(BF16)
    acc[1, slot, krows, :] += dot(probs_b, d2)
    acc[0, slot, krows, :] += dot(dscores, q2)
    dqt = dot(kw.T, dscores) * SCALE
    for h in range(HEADS):
        dq_v[slot, rows, h * HD : (h + 1) * HD] = dqt[:, h * HD : (h + 1) * HD].T.astype(BF16)


def kernel(
    n_ctx,
    n_head,
    q_hbm,
    do_hbm,
    k_hbm,
    v_hbm,
    doc_hbm,
    dq_v,
    dkv_v,
    stage,
    q_v,
    do_v,
    kv,
    acc,
    out_v,
    tail_out,
    tail_in,
    docs,
    stage_sem,
    load_sem,
    doc_sem,
    kv_send,
    kv_recv,
    relay_send,
    relay_recv,
    tail_send,
    tail_recv,
    out_send,
    out_recv,
    ready,
):
    c = lax.axis_index("ctx")
    x = lax.axis_index("head")
    is_first = c == 0
    is_last = c == n_ctx - 1
    first = jnp.where(is_first, 1, 0)
    row_start = lax.rem(c, ROW) == 0
    row_end = lax.rem(c, ROW) == ROW - 1
    early = jnp.logical_and(row_start, c > 0)
    late = jnp.logical_and(row_end, c < n_ctx - 1)
    lead = jnp.where(jnp.logical_or(early, late), 1, 0)

    barrier = pltpu.get_barrier_semaphore()

    def to_ctx(step):
        return (c + step, x)

    for d in range(1, n_head):
        pl.semaphore_signal(
            barrier, inc=1, device_id=(c, lax.rem(x + d, n_head)), device_id_type=MESH
        )

    @pl.when(c > 0)
    def _():
        pl.semaphore_signal(barrier, inc=1, device_id=to_ctx(-1), device_id_type=MESH)

    @pl.when(jnp.logical_not(row_end))
    def _():
        pl.semaphore_signal(barrier, inc=1, device_id=to_ctx(1), device_id_type=MESH)

    doc_copy = pltpu.make_async_copy(doc_hbm, docs, doc_sem)
    doc_copy.start()

    def kv_place(which, slot, block):
        return kv.at[which, slot, pl.ds(at_block(block + 2), BLK), :]

    staged = []
    for slot in range(2):
        for which, source in enumerate((k_hbm, v_hbm)):
            staged.append(
                pltpu.make_async_copy(
                    source.at[slot], stage.at[which, slot], stage_sem.at[which, slot]
                )
            )
            staged[-1].start()
            pltpu.make_async_copy(
                source.at[slot, :, pl.ds(at_block(x), HD)],
                kv_place(which, slot, x),
                kv_recv.at[which, slot, x],
            ).start()
    loads = []
    for slot in range(2):
        for i, (src, dst) in enumerate(((q_hbm, q_v), (do_hbm, do_v))):
            loads.append(
                pltpu.make_async_copy(src.at[slot], dst.at[slot], load_sem.at[i, slot])
            )
            loads[-1].start()
    acc[...] = jnp.zeros_like(acc)

    @pl.when(is_first)
    def _():
        kv[:, 0, 0:TAIL, :] = jnp.zeros((2, TAIL, HD), BF16)

    kk = lax.broadcasted_iota(jnp.int32, (BLK, HEADS * BLK), 0)
    qq = lax.broadcasted_iota(jnp.int32, (BLK, HEADS * BLK), 1) % BLK
    tri = jnp.where(kk <= qq, 0.0, -BIG).astype(F32)
    for copy in staged:
        copy.wait()

    partners = n_head - 1 + jnp.where(is_last, 0, 1) + jnp.where(row_start, 0, 1)
    pl.semaphore_wait(barrier, partners)

    @pl.when(late)
    def _():
        pl.semaphore_signal(ready, inc=1, device_id=to_ctx(1), device_id_type=MESH)

    sends = []
    for slot in range(2):
        for which in range(2):
            for d in (2, 1, 3):
                to = lax.rem(x + d, n_head)
                copy = pltpu.make_async_remote_copy(
                    src_ref=stage.at[which, slot, :, pl.ds(at_block(to), HD)],
                    dst_ref=kv_place(which, slot, x),
                    send_sem=kv_send.at[which, slot, d],
                    recv_sem=kv_recv.at[which, slot, x],
                    device_id=(c, to),
                    device_id_type=MESH,
                )
                copy.start()
                sends.append(copy)

    def wait_block(slot, block):
        for which in range(2):
            place = kv_place(which, slot, block)
            pltpu.make_async_copy(place, place, kv_recv.at[which, slot, block]).wait()

    def relay(slot, which, step):
        return pltpu.make_async_remote_copy(
            src_ref=kv.at[which, slot, pl.ds(SPAN, TAIL), :],
            dst_ref=kv.at[which, slot, pl.ds(0, TAIL), :],
            send_sem=relay_send.at[slot, which],
            recv_sem=relay_recv.at[slot, which],
            device_id=to_ctx(step),
            device_id_type=MESH,
        )

    def tail_copy(slot, step):
        return pltpu.make_async_remote_copy(
            src_ref=tail_out.at[slot],
            dst_ref=tail_in.at[slot],
            send_sem=tail_send.at[slot],
            recv_sem=tail_recv.at[slot],
            device_id=to_ctx(step),
            device_id_type=MESH,
        )

    def has(slot):
        if isinstance(slot, int):
            return jnp.logical_not(is_first) if slot == 0 else jnp.logical_not(is_last)
        return jnp.where(slot == 0, c > 0, c < n_ctx - 1)

    def send_tail(slot):
        tail_out[slot, 0] = (acc[0, slot, 0:TAIL, :] * SCALE).astype(BF16)
        tail_out[slot, 1] = acc[1, slot, 0:TAIL, :].astype(BF16)

        @pl.when(has(slot))
        def _():
            tail_copy(slot, 2 * slot - 1).start()

    def out_remote(slot, block):
        return pltpu.make_async_remote_copy(
            src_ref=out_v.at[slot, block],
            dst_ref=dkv_v.at[:, slot, :, pl.ds(at_block(x), HD)],
            send_sem=out_send.at[slot, block],
            recv_sem=out_recv.at[slot, x],
            device_id=(c, block),
            device_id_type=MESH,
        )

    def send_out(slot, block, extra=None):
        rows = pl.ds((block + 2) * BLK, BLK)
        for which in range(2):
            value = acc[which, slot, rows, :]
            if which == 0:
                value = value * SCALE
            if extra is not None:
                value = value + extra(which, block - 2)
            out_v[slot, block, which] = value.astype(BF16)

        @pl.when(x != block)
        def _():
            out_remote(slot, block).start()

        @pl.when(x == block)
        def _():
            place = dkv_v.at[:, slot, :, pl.ds(at_block(x), HD)]
            pltpu.make_async_copy(out_v.at[slot, block], place, out_recv.at[slot, x]).start()

    def span_of(slot):
        return jnp.where(slot == 0, c, 2 * n_ctx - 1 - c)

    tools = (q_v, do_v, dq_v, kv, acc, docs, tri)

    wait_block(0, 2)
    wait_block(0, 3)

    @pl.when(jnp.logical_not(is_last))
    def _():
        relay(0, 0, 1).start()
        relay(0, 1, 1).start()

    wait_block(0, 0)
    wait_block(0, 1)
    doc_copy.wait()
    loads[0].wait()
    loads[1].wait()
    block_grads(*tools, 0, span_of(0), 3, 4, 2)
    block_grads(*tools, 0, span_of(0), 2 - first, 3 - first, 2)
    for block in (2, 3, 0, 1):
        wait_block(1, block)

    @pl.when(early)
    def _():
        pl.semaphore_wait(ready, 1)

    @pl.when(jnp.logical_not(is_first))
    def _():
        relay(1, 0, -1).start()
        relay(1, 1, -1).start()

    @pl.when(is_last)
    def _():
        kv[:, 1, 0:TAIL, :] = kv[:, 0, SPAN : SPAN + TAIL, :]

    loads[2].wait()
    loads[3].wait()

    def front(slot):
        @pl.when(has(slot))
        def _():
            relay(slot, 0, 1).wait_recv()
            relay(slot, 1, 1).wait_recv()

        swap = jnp.where(slot == 0, first, 0)
        block_grads(*tools, slot, span_of(slot), 0, 0, 3)
        block_grads(*tools, slot, span_of(slot), 1 + swap, 1 + swap, 3)
        send_tail(slot)

    front(lead)
    front(1 - lead)
    send_out(0, 0)
    send_out(0, 1)
    send_out(1, 0)
    block_grads(*tools, 1, span_of(1), 3, 3, 3)

    def tail_arrives(slot):
        @pl.when(has(1 - slot))
        def _():
            tail_copy(slot, 1).wait_recv()

    def extra_first(which, i):
        arrived = tail_in[0, which, i * BLK : (i + 1) * BLK, :].astype(F32)
        mine = tail_out[1, which, i * BLK : (i + 1) * BLK, :].astype(F32)
        return jnp.where(is_last, mine, arrived)

    def extra_second(which, i):
        arrived = tail_in[1, which, i * BLK : (i + 1) * BLK, :].astype(F32)
        return jnp.where(is_first, 0.0, arrived)

    tail_arrives(0)
    send_out(0, 2, extra_first)
    send_out(0, 3, extra_first)
    block_grads(*tools, 1, span_of(1), 2, 3, 2)
    send_out(1, 1)
    tail_arrives(1)
    send_out(1, 2, extra_second)
    send_out(1, 3, extra_second)

    for copy in sends:
        copy.wait_send()
    for slot in range(2):

        @pl.when(has(1 - slot))
        def _():
            relay(slot, 0, 1).wait_send()
            relay(slot, 1, 1).wait_send()

        @pl.when(has(slot))
        def _():
            tail_copy(slot, 1).wait_send()

        for block in range(4):

            @pl.when(x != block)
            def _():
                out_remote(slot, block).wait_send()

            place = dkv_v.at[:, slot, :, pl.ds(block * HD, HD)]
            pltpu.make_async_copy(place, place, out_recv.at[slot, block]).wait()


def store_kernel(dq_v, dkv_v, dq_hbm, dk_hbm, dv_hbm, sem):
    copies = []
    for slot in range(2):
        for block in range(4):
            rows = pl.ds(block * BLK, BLK)
            copies.append((dq_v.at[slot, rows, :], dq_hbm.at[slot, rows, :]))
    copies.append((dkv_v.at[0], dk_hbm))
    copies.append((dkv_v.at[1], dv_hbm))
    started = [
        pltpu.make_async_copy(src, dst, sem.at[i]) for i, (src, dst) in enumerate(copies)
    ]
    for copy in started:
        copy.start()
    for copy in started:
        copy.wait()


def per_device(n_ctx, n_head, query, key, value, d_out, doc_start):
    hbm = pl.BlockSpec(memory_space=pltpu.HBM)
    vmem = pl.BlockSpec(memory_space=pltpu.VMEM)
    dma = pltpu.SemaphoreType.DMA
    dq, dkv = pl.pallas_call(
        functools.partial(kernel, n_ctx, n_head),
        out_shape=(
            jax.ShapeDtypeStruct((2, SPAN, HEADS * HD), BF16),
            jax.ShapeDtypeStruct((2, 2, BLK, n_head * HD), BF16),
        ),
        in_specs=[hbm] * 5,
        out_specs=(vmem, vmem),
        scratch_shapes=[
            pltpu.VMEM((2, 2, BLK, n_head * HD), BF16),
            pltpu.VMEM((2, SPAN, HEADS * HD), BF16),
            pltpu.VMEM((2, SPAN, HEADS * HD), BF16),
            pltpu.VMEM((2, 2, EXT, HD), BF16),
            pltpu.VMEM((2, 2, EXT, HD), F32),
            pltpu.VMEM((2, 4, 2, BLK, HD), BF16),
            pltpu.VMEM((2, 2, TAIL, HD), BF16),
            pltpu.VMEM((2, 2, TAIL, HD), BF16),
            pltpu.SMEM(doc_start.shape, jnp.int32),
            dma((2, 2)),
            dma((2, 2)),
            dma,
            dma((2, 2, 4)),
            dma((2, 2, 4)),
            dma((2, 2)),
            dma((2, 2)),
            dma((2,)),
            dma((2,)),
            dma((2, 4)),
            dma((2, 4)),
            pltpu.SemaphoreType.REGULAR,
        ],
        compiler_params=pltpu.CompilerParams(
            collective_id=0, has_side_effects=True, vmem_limit_bytes=40 << 20
        ),
    )(*[pltpu.with_memory_space_constraint(a, pltpu.HBM) for a in (query[0], d_out[0], key[0], value[0], doc_start)])
    d_query, d_key, d_value = pl.pallas_call(
        store_kernel,
        out_shape=(
            jax.ShapeDtypeStruct((2, SPAN, HEADS * HD), BF16),
            jax.ShapeDtypeStruct((2, BLK, n_head * HD), BF16),
            jax.ShapeDtypeStruct((2, BLK, n_head * HD), BF16),
        ),
        in_specs=[vmem, vmem],
        out_specs=(hbm, hbm, hbm),
        scratch_shapes=[dma((10,))],
        compiler_params=pltpu.CompilerParams(vmem_limit_bytes=1 << 20),
    )(dq, dkv)
    return d_query[None], d_key[None], d_value[None]


def solution(mesh):
    return jax.shard_map(
        functools.partial(per_device, mesh.shape["ctx"], mesh.shape["head"]),
        mesh=mesh,
        in_specs=(
            P("ctx", None, None, "head"),
            P("ctx", None, "head", None),
            P("ctx", None, "head", None),
            P("ctx", None, None, "head"),
            P(),
        ),
        out_specs=(
            P("ctx", None, None, "head"),
            P("ctx", None, "head", None),
            P("ctx", None, "head", None),
        ),
        check_vma=False,
    )
```

```python
import functools

import jax
import jax.numpy as jnp
from jax import lax
from jax.experimental import pallas as pl
from jax.experimental.pallas import tpu as pltpu
from jax.sharding import PartitionSpec as P

F32 = jnp.float32
BF16 = jnp.bfloat16
HD = 128
BLK = 128
HEADS = 8
SPAN = 512
TAIL = 256
ROW = 16
EXT = TAIL + SPAN
SCALE = HD**-0.5
SCALE_LOG2E = SCALE * 1.4426950408889634
BIG = 1e30
NT = (((1,), (1,)), ((), ()))
NN = (((1,), (0,)), ((), ()))
MESH = pl.DeviceIdType.MESH


def dot(a, b, dims=NN):
    return lax.dot_general(a, b, dims, preferred_element_type=F32)


def at_block(index):
    if isinstance(index, int):
        return index * BLK
    return pl.multiple_of(index * BLK, BLK)


def block_grads(q_v, do_v, dq_v, kv, acc, docs, tri, slot, span, qb, k0, nk):
    rows = pl.ds(at_block(qb), BLK)
    krows = pl.ds(at_block(k0), nk * BLK)
    kw = kv[0, slot, krows, :]
    vw = kv[1, slot, krows, :]
    g = span * 4 + qb
    hidden = docs[g]
    hide = [hidden]
    for back in range(1, nk - 1):
        hidden = hidden + docs[jnp.maximum(g - back, 0)]
        hide.append(hidden)
    subs = [jnp.where(x > 0, BIG, 0.0).astype(F32) for x in hide][::-1]
    qq = q_v[slot, rows, :]
    dd = do_v[slot, rows, :]
    q2 = jnp.concatenate([qq[:, h * HD : (h + 1) * HD] for h in range(HEADS)], axis=0)
    d2 = jnp.concatenate([dd[:, h * HD : (h + 1) * HD] for h in range(HEADS)], axis=0)
    scores = dot(kw, q2, NT)
    dprobs = dot(vw, d2, NT)
    parts = [scores[i * BLK : (i + 1) * BLK] for i in range(nk)]
    parts[-1] = parts[-1] + tri
    tops = [jnp.max(x, axis=0, keepdims=True) for x in parts]
    top = tops[-1]
    for i in range(nk - 1):
        top = jnp.maximum(top, tops[i] - subs[i])
    top = top * SCALE_LOG2E
    weights = []
    for i in range(nk):
        low = top if i == nk - 1 else top + subs[i]
        weights.append(jnp.exp2(parts[i] * SCALE_LOG2E - low))
    total = sum(jnp.sum(x, axis=0, keepdims=True) for x in weights)
    inverse = 1.0 / total
    weights = jnp.concatenate(weights, axis=0)
    probs_b = (weights * inverse).astype(BF16)
    delta = inverse * jnp.sum(weights * dprobs, axis=0, keepdims=True)
    dscores = (weights * inverse * (dprobs - delta)).astype(BF16)
    acc[1, slot, krows, :] += dot(probs_b, d2)
    acc[0, slot, krows, :] += dot(dscores, q2)
    dqt = dot(kw.T, dscores) * SCALE
    for h in range(HEADS):
        dq_v[slot, rows, h * HD : (h + 1) * HD] = dqt[:, h * HD : (h + 1) * HD].T.astype(BF16)


def kernel(
    n_ctx,
    n_head,
    q_hbm,
    do_hbm,
    k_hbm,
    v_hbm,
    doc_hbm,
    dq_v,
    dkv_v,
    stage,
    q_v,
    do_v,
    kv,
    acc,
    out_v,
    tail_out,
    tail_in,
    docs,
    stage_sem,
    load_sem,
    doc_sem,
    kv_send,
    kv_recv,
    relay_send,
    relay_recv,
    tail_send,
    tail_recv,
    out_send,
    out_recv,
    ready,
):
    c = lax.axis_index("ctx")
    x = lax.axis_index("head")
    is_first = c == 0
    is_last = c == n_ctx - 1
    first = jnp.where(is_first, 1, 0)
    row_start = lax.rem(c, ROW) == 0
    row_end = lax.rem(c, ROW) == ROW - 1
    early = jnp.logical_and(row_start, c > 0)
    late = jnp.logical_and(row_end, c < n_ctx - 1)
    lead = jnp.where(jnp.logical_or(early, late), 1, 0)

    barrier = pltpu.get_barrier_semaphore()

    def to_ctx(step):
        return (c + step, x)

    for d in range(1, n_head):
        pl.semaphore_signal(
            barrier, inc=1, device_id=(c, lax.rem(x + d, n_head)), device_id_type=MESH
        )

    @pl.when(c > 0)
    def _():
        pl.semaphore_signal(barrier, inc=1, device_id=to_ctx(-1), device_id_type=MESH)

    @pl.when(jnp.logical_not(row_end))
    def _():
        pl.semaphore_signal(barrier, inc=1, device_id=to_ctx(1), device_id_type=MESH)

    doc_copy = pltpu.make_async_copy(doc_hbm, docs, doc_sem)
    doc_copy.start()

    def kv_place(slot, block):
        return kv.at[:, slot, pl.ds(at_block(block + 2), BLK), :]

    staged = []
    for slot in range(2):
        for which, source in enumerate((k_hbm, v_hbm)):
            staged.append(
                pltpu.make_async_copy(
                    source.at[slot], stage.at[which, slot], stage_sem.at[which, slot]
                )
            )
            staged[-1].start()
    loads = []
    for slot in range(2):
        for i, (src, dst) in enumerate(((q_hbm, q_v), (do_hbm, do_v))):
            loads.append(
                pltpu.make_async_copy(src.at[slot], dst.at[slot], load_sem.at[i, slot])
            )
            loads[-1].start()
    acc[...] = jnp.zeros_like(acc)

    @pl.when(is_first)
    def _():
        kv[:, 0, 0:TAIL, :] = jnp.zeros((2, TAIL, HD), BF16)

    kk = lax.broadcasted_iota(jnp.int32, (BLK, HEADS * BLK), 0)
    qq = lax.broadcasted_iota(jnp.int32, (BLK, HEADS * BLK), 1) % BLK
    tri = jnp.where(kk <= qq, 0.0, -BIG).astype(F32)
    for copy in staged:
        copy.wait()
    for which in range(2):
        for slot in range(2):
            mine = stage[which, slot, :, pl.ds(at_block(x), HD)]
            kv[which, slot, pl.ds(at_block(x + 2), BLK), :] = mine

    partners = n_head - 1 + jnp.where(is_last, 0, 1) + jnp.where(row_start, 0, 1)
    pl.semaphore_wait(barrier, partners)

    @pl.when(late)
    def _():
        pl.semaphore_signal(ready, inc=1, device_id=to_ctx(1), device_id_type=MESH)

    sends = []
    for slot in range(2):
        for d in (2, 1, 3):
            to = lax.rem(x + d, n_head)
            copy = pltpu.make_async_remote_copy(
                src_ref=stage.at[:, slot, :, pl.ds(at_block(to), HD)],
                dst_ref=kv_place(slot, x),
                send_sem=kv_send.at[slot, d],
                recv_sem=kv_recv.at[slot, x],
                device_id=(c, to),
                device_id_type=MESH,
            )
            copy.start()
            sends.append(copy)

    def wait_kv(slot, block):
        @pl.when(x != block)
        def _():
            place = kv_place(slot, block)
            pltpu.make_async_copy(place, place, kv_recv.at[slot, block]).wait()

    def relay(slot, step):
        return pltpu.make_async_remote_copy(
            src_ref=kv.at[:, slot, pl.ds(SPAN, TAIL), :],
            dst_ref=kv.at[:, slot, pl.ds(0, TAIL), :],
            send_sem=relay_send.at[slot],
            recv_sem=relay_recv.at[slot],
            device_id=to_ctx(step),
            device_id_type=MESH,
        )

    def tail_copy(slot, i, step):
        return pltpu.make_async_remote_copy(
            src_ref=tail_out.at[slot, i],
            dst_ref=tail_in.at[slot, i],
            send_sem=tail_send.at[slot, i],
            recv_sem=tail_recv.at[slot, i],
            device_id=to_ctx(step),
            device_id_type=MESH,
        )

    def has(slot):
        if isinstance(slot, int):
            return jnp.logical_not(is_first) if slot == 0 else jnp.logical_not(is_last)
        return jnp.where(slot == 0, c > 0, c < n_ctx - 1)

    def send_tail(slot, i):
        rows = pl.ds(i * BLK, BLK)
        tail_out[slot, i, 0] = (acc[0, slot, rows, :] * SCALE).astype(BF16)
        tail_out[slot, i, 1] = acc[1, slot, rows, :].astype(BF16)

        @pl.when(has(slot))
        def _():
            tail_copy(slot, i, 2 * slot - 1).start()

    def out_remote(slot, block):
        return pltpu.make_async_remote_copy(
            src_ref=out_v.at[slot, block],
            dst_ref=dkv_v.at[:, slot, :, pl.ds(at_block(x), HD)],
            send_sem=out_send.at[slot, block],
            recv_sem=out_recv.at[slot, x],
            device_id=(c, block),
            device_id_type=MESH,
        )

    def send_out(slot, block, extra=None):
        rows = pl.ds((block + 2) * BLK, BLK)
        for which in range(2):
            value = acc[which, slot, rows, :]
            if which == 0:
                value = value * SCALE
            if extra is not None:
                value = value + extra(which, block - 2)
            out_v[slot, block, which] = value.astype(BF16)

        @pl.when(x != block)
        def _():
            out_remote(slot, block).start()

        @pl.when(x == block)
        def _():
            place = dkv_v.at[:, slot, :, pl.ds(at_block(x), HD)]
            pltpu.make_async_copy(out_v.at[slot, block], place, out_recv.at[slot, x]).start()

    def span_of(slot):
        return jnp.where(slot == 0, c, 2 * n_ctx - 1 - c)

    tools = (q_v, do_v, dq_v, kv, acc, docs, tri)

    wait_kv(0, 3)
    wait_kv(0, 2)

    @pl.when(jnp.logical_not(is_last))
    def _():
        relay(0, 1).start()

    doc_copy.wait()
    loads[0].wait()
    loads[1].wait()
    wait_kv(0, 1)
    wait_kv(0, 0)
    block_grads(*tools, 0, span_of(0), 3, 4, 2)
    block_grads(*tools, 0, span_of(0), 2 - first, 3 - first, 2)

    @pl.when(early)
    def _():
        pl.semaphore_wait(ready, 1)

    wait_kv(1, 3)
    wait_kv(1, 2)

    @pl.when(jnp.logical_not(is_first))
    def _():
        relay(1, -1).start()

    wait_kv(1, 1)
    wait_kv(1, 0)

    @pl.when(is_last)
    def _():
        kv[:, 1, 0:TAIL, :] = kv[:, 0, SPAN : SPAN + TAIL, :]

    loads[2].wait()
    loads[3].wait()

    def front(slot):
        @pl.when(has(slot))
        def _():
            relay(slot, 1).wait_recv()

        swap = jnp.where(slot == 0, first, 0)
        block_grads(*tools, slot, span_of(slot), 0, 0, 3)
        block_grads(*tools, slot, span_of(slot), 1 + swap, 1 + swap, 3)
        send_tail(slot, 0)
        send_tail(slot, 1)

    front(lead)

    @pl.when(lead == 0)
    def _():
        send_out(0, 0)
        send_out(0, 1)

    @pl.when(lead == 1)
    def _():
        send_out(1, 0)

    front(1 - lead)

    @pl.when(lead == 1)
    def _():
        send_out(0, 0)
        send_out(0, 1)

    @pl.when(lead == 0)
    def _():
        send_out(1, 0)

    def tail_arrives(slot, i):
        @pl.when(has(1 - slot))
        def _():
            tail_copy(slot, i, 1).wait_recv()

    def extra_first(which, i):
        arrived = tail_in[0, i, which].astype(F32)
        mine = tail_out[1, i, which].astype(F32)
        return jnp.where(is_last, mine, arrived)

    def extra_second(which, i):
        return jnp.where(is_first, 0.0, tail_in[1, i, which].astype(F32))

    for i in range(2):
        tail_arrives(0, i)
        send_out(0, 2 + i, extra_first)

    @pl.when(is_first)
    def _():
        block_grads(*tools, 1, span_of(1), 2, 3, 2)
        block_grads(*tools, 1, span_of(1), 3, 3, 3)

    @pl.when(jnp.logical_not(is_first))
    def _():
        block_grads(*tools, 1, span_of(1), 2, 3, 2)
        block_grads(*tools, 1, span_of(1), 3, 4, 2)

    send_out(1, 1)

    for i in range(2):
        tail_arrives(1, i)
        send_out(1, 2 + i, extra_second)

    for copy in sends:
        copy.wait_send()
    for slot in range(2):

        @pl.when(has(1 - slot))
        def _():
            relay(slot, 1).wait_send()

        @pl.when(has(slot))
        def _():
            tail_copy(slot, 0, 1).wait_send()
            tail_copy(slot, 1, 1).wait_send()

        for block in range(4):

            @pl.when(x != block)
            def _():
                out_remote(slot, block).wait_send()

            place = dkv_v.at[:, slot, :, pl.ds(block * HD, HD)]
            pltpu.make_async_copy(place, place, out_recv.at[slot, block]).wait()


def store_kernel(dq_v, dkv_v, dq_hbm, dk_hbm, dv_hbm, sem):
    copies = []
    for slot in range(2):
        for block in range(4):
            rows = pl.ds(block * BLK, BLK)
            copies.append((dq_v.at[slot, rows, :], dq_hbm.at[slot, rows, :]))
    copies.append((dkv_v.at[0], dk_hbm))
    copies.append((dkv_v.at[1], dv_hbm))
    started = [
        pltpu.make_async_copy(src, dst, sem.at[i]) for i, (src, dst) in enumerate(copies)
    ]
    for copy in started:
        copy.start()
    for copy in started:
        copy.wait()


def per_device(n_ctx, n_head, query, key, value, d_out, doc_start):
    hbm = pl.BlockSpec(memory_space=pltpu.HBM)
    vmem = pl.BlockSpec(memory_space=pltpu.VMEM)
    dma = pltpu.SemaphoreType.DMA
    dq, dkv = pl.pallas_call(
        functools.partial(kernel, n_ctx, n_head),
        out_shape=(
            jax.ShapeDtypeStruct((2, SPAN, HEADS * HD), BF16),
            jax.ShapeDtypeStruct((2, 2, BLK, n_head * HD), BF16),
        ),
        in_specs=[hbm] * 5,
        out_specs=(vmem, vmem),
        scratch_shapes=[
            pltpu.VMEM((2, 2, BLK, n_head * HD), BF16),
            pltpu.VMEM((2, SPAN, HEADS * HD), BF16),
            pltpu.VMEM((2, SPAN, HEADS * HD), BF16),
            pltpu.VMEM((2, 2, EXT, HD), BF16),
            pltpu.VMEM((2, 2, EXT, HD), F32),
            pltpu.VMEM((2, 4, 2, BLK, HD), BF16),
            pltpu.VMEM((2, 2, 2, BLK, HD), BF16),
            pltpu.VMEM((2, 2, 2, BLK, HD), BF16),
            pltpu.SMEM(doc_start.shape, jnp.int32),
            dma((2, 2)),
            dma((2, 2)),
            dma,
            dma((2, 4)),
            dma((2, 4)),
            dma((2,)),
            dma((2,)),
            dma((2, 2)),
            dma((2, 2)),
            dma((2, 4)),
            dma((2, 4)),
            pltpu.SemaphoreType.REGULAR,
        ],
        compiler_params=pltpu.CompilerParams(
            collective_id=0, has_side_effects=True, vmem_limit_bytes=40 << 20
        ),
    )(*[
            pltpu.with_memory_space_constraint(a, pltpu.HBM)
            for a in (query[0], d_out[0], key[0], value[0], doc_start)
        ])
    d_query, d_key, d_value = pl.pallas_call(
        store_kernel,
        out_shape=(
            jax.ShapeDtypeStruct((2, SPAN, HEADS * HD), BF16),
            jax.ShapeDtypeStruct((2, BLK, n_head * HD), BF16),
            jax.ShapeDtypeStruct((2, BLK, n_head * HD), BF16),
        ),
        in_specs=[vmem, vmem],
        out_specs=(hbm, hbm, hbm),
        scratch_shapes=[dma((10,))],
        compiler_params=pltpu.CompilerParams(vmem_limit_bytes=1 << 20),
    )(dq, dkv)
    return d_query[None], d_key[None], d_value[None]


def solution(mesh):
    return jax.shard_map(
        functools.partial(per_device, mesh.shape["ctx"], mesh.shape["head"]),
        mesh=mesh,
        in_specs=(
            P("ctx", None, None, "head"),
            P("ctx", None, "head", None),
            P("ctx", None, "head", None),
            P("ctx", None, None, "head"),
            P(),
        ),
        out_specs=(
            P("ctx", None, None, "head"),
            P("ctx", None, "head", None),
            P("ctx", None, "head", None),
        ),
        check_vma=False,
    )
```

```python
import functools

import jax
import jax.numpy as jnp
from jax import lax
from jax.experimental import pallas as pl
from jax.experimental.pallas import tpu as pltpu
from jax.sharding import PartitionSpec as P

F32 = jnp.float32
BF16 = jnp.bfloat16
HD = 128
BLK = 128
HEADS = 8
SPAN = 512
TAIL = 256
ROW = 16
EXT = TAIL + SPAN
SCALE = HD**-0.5
SCALE_LOG2E = SCALE * 1.4426950408889634
BIG = 1e30
NT = (((1,), (1,)), ((), ()))
NN = (((1,), (0,)), ((), ()))
MESH = pl.DeviceIdType.MESH


def dot(a, b, dims=NN):
    return lax.dot_general(a, b, dims, preferred_element_type=F32)


def at_block(index):
    if isinstance(index, int):
        return index * BLK
    return pl.multiple_of(index * BLK, BLK)


def block_grads(q_v, do_v, dq_v, kv, acc, docs, tri, slot, span, qb, k0, nk):
    rows = pl.ds(at_block(qb), BLK)
    krows = pl.ds(at_block(k0), nk * BLK)
    kw = kv[0, slot, krows, :]
    vw = kv[1, slot, krows, :]
    g = span * 4 + qb
    hidden = docs[g]
    hide = [hidden]
    for back in range(1, nk - 1):
        hidden = hidden + docs[jnp.maximum(g - back, 0)]
        hide.append(hidden)
    subs = [jnp.where(x > 0, BIG, 0.0).astype(F32) for x in hide][::-1]
    qq = q_v[slot, rows, :]
    dd = do_v[slot, rows, :]
    q2 = jnp.concatenate([qq[:, h * HD : (h + 1) * HD] for h in range(HEADS)], axis=0)
    d2 = jnp.concatenate([dd[:, h * HD : (h + 1) * HD] for h in range(HEADS)], axis=0)
    scores = dot(kw, q2, NT)
    dprobs = dot(vw, d2, NT)
    parts = [scores[i * BLK : (i + 1) * BLK] for i in range(nk)]
    parts[-1] = parts[-1] + tri
    tops = [jnp.max(x, axis=0, keepdims=True) for x in parts]
    top = tops[-1]
    for i in range(nk - 1):
        top = jnp.maximum(top, tops[i] - subs[i])
    top = top * SCALE_LOG2E
    weights = []
    for i in range(nk):
        low = top if i == nk - 1 else top + subs[i]
        weights.append(jnp.exp2(parts[i] * SCALE_LOG2E - low))
    total = sum(jnp.sum(x, axis=0, keepdims=True) for x in weights)
    inverse = 1.0 / total
    weights = jnp.concatenate(weights, axis=0)
    probs_b = (weights * inverse).astype(BF16)
    delta = inverse * jnp.sum(weights * dprobs, axis=0, keepdims=True)
    dscores = (weights * inverse * (dprobs - delta)).astype(BF16)
    acc[1, slot, krows, :] += dot(probs_b, d2)
    acc[0, slot, krows, :] += dot(dscores, q2)
    dqt = dot(kw.T, dscores) * SCALE
    for h in range(HEADS):
        dq_v[slot, rows, h * HD : (h + 1) * HD] = dqt[:, h * HD : (h + 1) * HD].T.astype(BF16)


def kernel(
    n_ctx,
    n_head,
    q_hbm,
    do_hbm,
    k_hbm,
    v_hbm,
    doc_hbm,
    dq_v,
    dkv_v,
    stage,
    q_v,
    do_v,
    kv,
    acc,
    out_v,
    tail_out,
    tail_in,
    docs,
    stage_sem,
    load_sem,
    doc_sem,
    kv_send,
    kv_recv,
    relay_send,
    relay_recv,
    tail_send,
    tail_recv,
    out_send,
    out_recv,
    ready,
):
    c = lax.axis_index("ctx")
    x = lax.axis_index("head")
    is_first = c == 0
    is_last = c == n_ctx - 1
    first = jnp.where(is_first, 1, 0)
    row_start = lax.rem(c, ROW) == 0
    row_end = lax.rem(c, ROW) == ROW - 1
    early = jnp.logical_and(row_start, c > 0)
    late = jnp.logical_and(row_end, c < n_ctx - 1)
    lead = jnp.where(jnp.logical_or(early, late), 1, 0)

    barrier = pltpu.get_barrier_semaphore()

    def to_ctx(step):
        return (c + step, x)

    for d in range(1, n_head):
        pl.semaphore_signal(
            barrier, inc=1, device_id=(c, lax.rem(x + d, n_head)), device_id_type=MESH
        )

    @pl.when(c > 0)
    def _():
        pl.semaphore_signal(barrier, inc=1, device_id=to_ctx(-1), device_id_type=MESH)

    @pl.when(jnp.logical_not(row_end))
    def _():
        pl.semaphore_signal(barrier, inc=1, device_id=to_ctx(1), device_id_type=MESH)

    doc_copy = pltpu.make_async_copy(doc_hbm, docs, doc_sem)
    doc_copy.start()

    def kv_place(slot, block):
        return kv.at[:, slot, pl.ds(at_block(block + 2), BLK), :]

    staged = []
    for slot in range(2):
        for which, source in enumerate((k_hbm, v_hbm)):
            staged.append(
                pltpu.make_async_copy(
                    source.at[slot], stage.at[which, slot], stage_sem.at[which, slot]
                )
            )
            staged[-1].start()
    for copy in staged:
        copy.wait()
    partners = n_head - 1 + jnp.where(is_last, 0, 1) + jnp.where(row_start, 0, 1)
    pl.semaphore_wait(barrier, partners)

    @pl.when(late)
    def _():
        pl.semaphore_signal(ready, inc=1, device_id=to_ctx(1), device_id_type=MESH)

    sends = []
    for slot in range(2):
        for d in (2, 1, 3):
            to = lax.rem(x + d, n_head)
            copy = pltpu.make_async_remote_copy(
                src_ref=stage.at[:, slot, :, pl.ds(at_block(to), HD)],
                dst_ref=kv_place(slot, x),
                send_sem=kv_send.at[slot, d],
                recv_sem=kv_recv.at[slot, x],
                device_id=(c, to),
                device_id_type=MESH,
            )
            copy.start()
            sends.append(copy)

    loads = []
    for slot in range(2):
        for i, (src, dst) in enumerate(((q_hbm, q_v), (do_hbm, do_v))):
            loads.append(
                pltpu.make_async_copy(src.at[slot], dst.at[slot], load_sem.at[i, slot])
            )
            loads[-1].start()
    for which in range(2):
        for slot in range(2):
            mine = stage[which, slot, :, pl.ds(at_block(x), HD)]
            kv[which, slot, pl.ds(at_block(x + 2), BLK), :] = mine

    acc[...] = jnp.zeros_like(acc)

    @pl.when(is_first)
    def _():
        kv[:, 0, 0:TAIL, :] = jnp.zeros((2, TAIL, HD), BF16)

    kk = lax.broadcasted_iota(jnp.int32, (BLK, HEADS * BLK), 0)
    qq = lax.broadcasted_iota(jnp.int32, (BLK, HEADS * BLK), 1) % BLK
    tri = jnp.where(kk <= qq, 0.0, -BIG).astype(F32)

    def wait_kv(slot, block):
        @pl.when(x != block)
        def _():
            place = kv_place(slot, block)
            pltpu.make_async_copy(place, place, kv_recv.at[slot, block]).wait()

    def relay(slot, step):
        return pltpu.make_async_remote_copy(
            src_ref=kv.at[:, slot, pl.ds(SPAN, TAIL), :],
            dst_ref=kv.at[:, slot, pl.ds(0, TAIL), :],
            send_sem=relay_send.at[slot],
            recv_sem=relay_recv.at[slot],
            device_id=to_ctx(step),
            device_id_type=MESH,
        )

    def tail_copy(slot, i, step):
        return pltpu.make_async_remote_copy(
            src_ref=tail_out.at[slot, i],
            dst_ref=tail_in.at[slot, i],
            send_sem=tail_send.at[slot, i],
            recv_sem=tail_recv.at[slot, i],
            device_id=to_ctx(step),
            device_id_type=MESH,
        )

    def has(slot):
        if isinstance(slot, int):
            return jnp.logical_not(is_first) if slot == 0 else jnp.logical_not(is_last)
        return jnp.where(slot == 0, c > 0, c < n_ctx - 1)

    def send_tail(slot, i):
        rows = pl.ds(i * BLK, BLK)
        tail_out[slot, i, 0] = (acc[0, slot, rows, :] * SCALE).astype(BF16)
        tail_out[slot, i, 1] = acc[1, slot, rows, :].astype(BF16)

        @pl.when(has(slot))
        def _():
            tail_copy(slot, i, 2 * slot - 1).start()

    def out_remote(slot, block):
        return pltpu.make_async_remote_copy(
            src_ref=out_v.at[slot, block],
            dst_ref=dkv_v.at[:, slot, :, pl.ds(at_block(x), HD)],
            send_sem=out_send.at[slot, block],
            recv_sem=out_recv.at[slot, x],
            device_id=(c, block),
            device_id_type=MESH,
        )

    def send_out(slot, block, extra=None):
        rows = pl.ds((block + 2) * BLK, BLK)
        for which in range(2):
            value = acc[which, slot, rows, :]
            if which == 0:
                value = value * SCALE
            if extra is not None:
                value = value + extra(which, block - 2)
            out_v[slot, block, which] = value.astype(BF16)

        @pl.when(x != block)
        def _():
            out_remote(slot, block).start()

        @pl.when(x == block)
        def _():
            place = dkv_v.at[:, slot, :, pl.ds(at_block(x), HD)]
            pltpu.make_async_copy(out_v.at[slot, block], place, out_recv.at[slot, x]).start()

    def span_of(slot):
        return jnp.where(slot == 0, c, 2 * n_ctx - 1 - c)

    tools = (q_v, do_v, dq_v, kv, acc, docs, tri)

    wait_kv(0, 3)
    wait_kv(0, 2)

    @pl.when(jnp.logical_not(is_last))
    def _():
        relay(0, 1).start()

    doc_copy.wait()
    loads[0].wait()
    loads[1].wait()
    wait_kv(0, 1)
    wait_kv(0, 0)
    block_grads(*tools, 0, span_of(0), 3, 4, 2)
    block_grads(*tools, 0, span_of(0), 2 - first, 3 - first, 2)

    @pl.when(early)
    def _():
        pl.semaphore_wait(ready, 1)

    wait_kv(1, 3)
    wait_kv(1, 2)

    @pl.when(jnp.logical_not(is_first))
    def _():
        relay(1, -1).start()

    wait_kv(1, 1)
    wait_kv(1, 0)

    @pl.when(is_last)
    def _():
        kv[:, 1, 0:TAIL, :] = kv[:, 0, SPAN : SPAN + TAIL, :]

    loads[2].wait()
    loads[3].wait()

    def front(slot):
        @pl.when(has(slot))
        def _():
            relay(slot, 1).wait_recv()

        swap = jnp.where(slot == 0, first, 0)
        block_grads(*tools, slot, span_of(slot), 0, 0, 3)
        block_grads(*tools, slot, span_of(slot), 1 + swap, 1 + swap, 3)
        send_tail(slot, 0)
        send_tail(slot, 1)

    front(lead)

    @pl.when(lead == 0)
    def _():
        send_out(0, 0)
        send_out(0, 1)

    @pl.when(lead == 1)
    def _():
        send_out(1, 0)

    front(1 - lead)

    @pl.when(lead == 1)
    def _():
        send_out(0, 0)
        send_out(0, 1)

    @pl.when(lead == 0)
    def _():
        send_out(1, 0)

    def tail_arrives(slot, i):
        @pl.when(has(1 - slot))
        def _():
            tail_copy(slot, i, 1).wait_recv()

    def extra_first(which, i):
        arrived = tail_in[0, i, which].astype(F32)
        mine = tail_out[1, i, which].astype(F32)
        return jnp.where(is_last, mine, arrived)

    def extra_second(which, i):
        return jnp.where(is_first, 0.0, tail_in[1, i, which].astype(F32))

    for i in range(2):
        tail_arrives(0, i)
        send_out(0, 2 + i, extra_first)

    @pl.when(is_first)
    def _():
        block_grads(*tools, 1, span_of(1), 2, 3, 2)
        block_grads(*tools, 1, span_of(1), 3, 3, 3)

    @pl.when(jnp.logical_not(is_first))
    def _():
        block_grads(*tools, 1, span_of(1), 2, 3, 2)
        block_grads(*tools, 1, span_of(1), 3, 4, 2)

    send_out(1, 1)

    for i in range(2):
        tail_arrives(1, i)
        send_out(1, 2 + i, extra_second)

    for copy in sends:
        copy.wait_send()
    for slot in range(2):

        @pl.when(has(1 - slot))
        def _():
            relay(slot, 1).wait_send()

        @pl.when(has(slot))
        def _():
            tail_copy(slot, 0, 1).wait_send()
            tail_copy(slot, 1, 1).wait_send()

        for block in range(4):

            @pl.when(x != block)
            def _():
                out_remote(slot, block).wait_send()

            place = dkv_v.at[:, slot, :, pl.ds(block * HD, HD)]
            pltpu.make_async_copy(place, place, out_recv.at[slot, block]).wait()


def store_kernel(dq_v, dkv_v, dq_hbm, dk_hbm, dv_hbm, sem):
    copies = []
    for slot in range(2):
        for block in range(4):
            rows = pl.ds(block * BLK, BLK)
            copies.append((dq_v.at[slot, rows, :], dq_hbm.at[slot, rows, :]))
    copies.append((dkv_v.at[0], dk_hbm))
    copies.append((dkv_v.at[1], dv_hbm))
    started = [
        pltpu.make_async_copy(src, dst, sem.at[i]) for i, (src, dst) in enumerate(copies)
    ]
    for copy in started:
        copy.start()
    for copy in started:
        copy.wait()


def per_device(n_ctx, n_head, query, key, value, d_out, doc_start):
    hbm = pl.BlockSpec(memory_space=pltpu.HBM)
    vmem = pl.BlockSpec(memory_space=pltpu.VMEM)
    dma = pltpu.SemaphoreType.DMA
    dq, dkv = pl.pallas_call(
        functools.partial(kernel, n_ctx, n_head),
        out_shape=(
            jax.ShapeDtypeStruct((2, SPAN, HEADS * HD), BF16),
            jax.ShapeDtypeStruct((2, 2, BLK, n_head * HD), BF16),
        ),
        in_specs=[hbm] * 5,
        out_specs=(vmem, vmem),
        scratch_shapes=[
            pltpu.VMEM((2, 2, BLK, n_head * HD), BF16),
            pltpu.VMEM((2, SPAN, HEADS * HD), BF16),
            pltpu.VMEM((2, SPAN, HEADS * HD), BF16),
            pltpu.VMEM((2, 2, EXT, HD), BF16),
            pltpu.VMEM((2, 2, EXT, HD), F32),
            pltpu.VMEM((2, 4, 2, BLK, HD), BF16),
            pltpu.VMEM((2, 2, 2, BLK, HD), BF16),
            pltpu.VMEM((2, 2, 2, BLK, HD), BF16),
            pltpu.SMEM(doc_start.shape, jnp.int32),
            dma((2, 2)),
            dma((2, 2)),
            dma,
            dma((2, 4)),
            dma((2, 4)),
            dma((2,)),
            dma((2,)),
            dma((2, 2)),
            dma((2, 2)),
            dma((2, 4)),
            dma((2, 4)),
            pltpu.SemaphoreType.REGULAR,
        ],
        compiler_params=pltpu.CompilerParams(
            collective_id=0, has_side_effects=True, vmem_limit_bytes=40 << 20
        ),
    )(*[
            pltpu.with_memory_space_constraint(a, pltpu.HBM)
            for a in (query[0], d_out[0], key[0], value[0], doc_start)
        ])
    d_query, d_key, d_value = pl.pallas_call(
        store_kernel,
        out_shape=(
            jax.ShapeDtypeStruct((2, SPAN, HEADS * HD), BF16),
            jax.ShapeDtypeStruct((2, BLK, n_head * HD), BF16),
            jax.ShapeDtypeStruct((2, BLK, n_head * HD), BF16),
        ),
        in_specs=[vmem, vmem],
        out_specs=(hbm, hbm, hbm),
        scratch_shapes=[dma((10,))],
        compiler_params=pltpu.CompilerParams(vmem_limit_bytes=1 << 20),
    )(dq, dkv)
    return d_query[None], d_key[None], d_value[None]


def solution(mesh):
    return jax.shard_map(
        functools.partial(per_device, mesh.shape["ctx"], mesh.shape["head"]),
        mesh=mesh,
        in_specs=(
            P("ctx", None, None, "head"),
            P("ctx", None, "head", None),
            P("ctx", None, "head", None),
            P("ctx", None, None, "head"),
            P(),
        ),
        out_specs=(
            P("ctx", None, None, "head"),
            P("ctx", None, "head", None),
            P("ctx", None, "head", None),
        ),
        check_vma=False,
    )
```

```python
import functools

import jax
import jax.numpy as jnp
from jax import lax
from jax.experimental import pallas as pl
from jax.experimental.pallas import tpu as pltpu
from jax.sharding import PartitionSpec as P

F32 = jnp.float32
BF16 = jnp.bfloat16
HD = 128
BLK = 128
HEADS = 8
SPAN = 512
TAIL = 256
ROW = 16
EXT = TAIL + SPAN
SCALE = HD**-0.5
SCALE_LOG2E = SCALE * 1.4426950408889634
BIG = 1e30
NT = (((1,), (1,)), ((), ()))
NN = (((1,), (0,)), ((), ()))
MESH = pl.DeviceIdType.MESH


def dot(a, b, dims=NN):
    return lax.dot_general(a, b, dims, preferred_element_type=F32)


def at_block(index):
    if isinstance(index, int):
        return index * BLK
    return pl.multiple_of(index * BLK, BLK)


def block_grads(q_v, do_v, dq_v, kv, acc, docs, tri, slot, span, qb, k0, nk):
    rows = pl.ds(at_block(qb), BLK)
    krows = pl.ds(at_block(k0), nk * BLK)
    kw = kv[0, slot, krows, :]
    vw = kv[1, slot, krows, :]
    g = span * 4 + qb
    hidden = docs[g]
    hide = [hidden]
    for back in range(1, nk - 1):
        hidden = hidden + docs[jnp.maximum(g - back, 0)]
        hide.append(hidden)
    subs = [jnp.where(x > 0, BIG, 0.0).astype(F32) for x in hide][::-1]
    qq = q_v[slot, rows, :]
    dd = do_v[slot, rows, :]
    q2 = jnp.concatenate([qq[:, h * HD : (h + 1) * HD] for h in range(HEADS)], axis=0)
    d2 = jnp.concatenate([dd[:, h * HD : (h + 1) * HD] for h in range(HEADS)], axis=0)
    scores = dot(kw, q2, NT)
    dprobs = dot(vw, d2, NT)
    parts = [scores[i * BLK : (i + 1) * BLK] for i in range(nk)]
    parts[-1] = parts[-1] + tri
    tops = [jnp.max(x, axis=0, keepdims=True) for x in parts]
    top = tops[-1]
    for i in range(nk - 1):
        top = jnp.maximum(top, tops[i] - subs[i])
    top = top * SCALE_LOG2E
    weights = []
    for i in range(nk):
        low = top if i == nk - 1 else top + subs[i]
        weights.append(jnp.exp2(parts[i] * SCALE_LOG2E - low))
    total = sum(jnp.sum(x, axis=0, keepdims=True) for x in weights)
    inverse = 1.0 / total
    weights = jnp.concatenate(weights, axis=0)
    probs_b = (weights * inverse).astype(BF16)
    delta = inverse * jnp.sum(weights * dprobs, axis=0, keepdims=True)
    dscores = probs_b * (dprobs - delta).astype(BF16)
    acc[1, slot, krows, :] += dot(probs_b, d2)
    acc[0, slot, krows, :] += dot(dscores, q2)
    dqt = dot(kw.T, dscores) * SCALE
    for h in range(HEADS):
        dq_v[slot, rows, h * HD : (h + 1) * HD] = dqt[:, h * HD : (h + 1) * HD].T.astype(BF16)


def kernel(
    n_ctx,
    n_head,
    q_hbm,
    do_hbm,
    k_hbm,
    v_hbm,
    doc_hbm,
    dq_v,
    dkv_v,
    stage,
    q_v,
    do_v,
    kv,
    acc,
    out_v,
    tail_out,
    tail_in,
    docs,
    stage_sem,
    load_sem,
    doc_sem,
    kv_send,
    kv_recv,
    relay_send,
    relay_recv,
    tail_send,
    tail_recv,
    out_send,
    out_recv,
    ready,
):
    c = lax.axis_index("ctx")
    x = lax.axis_index("head")
    is_first = c == 0
    is_last = c == n_ctx - 1
    first = jnp.where(is_first, 1, 0)
    row_start = lax.rem(c, ROW) == 0
    row_end = lax.rem(c, ROW) == ROW - 1
    early = jnp.logical_and(row_start, c > 0)
    late = jnp.logical_and(row_end, c < n_ctx - 1)
    lead = jnp.where(jnp.logical_or(early, late), 1, 0)

    barrier = pltpu.get_barrier_semaphore()

    def to_ctx(step):
        return (c + step, x)

    for d in range(1, n_head):
        pl.semaphore_signal(
            barrier, inc=1, device_id=(c, lax.rem(x + d, n_head)), device_id_type=MESH
        )

    @pl.when(c > 0)
    def _():
        pl.semaphore_signal(barrier, inc=1, device_id=to_ctx(-1), device_id_type=MESH)

    @pl.when(jnp.logical_not(row_end))
    def _():
        pl.semaphore_signal(barrier, inc=1, device_id=to_ctx(1), device_id_type=MESH)

    doc_copy = pltpu.make_async_copy(doc_hbm, docs, doc_sem)
    doc_copy.start()

    def kv_place(slot, block):
        return kv.at[:, slot, pl.ds(at_block(block + 2), BLK), :]

    staged = []
    for slot in range(2):
        for which, source in enumerate((k_hbm, v_hbm)):
            staged.append(
                pltpu.make_async_copy(
                    source.at[slot], stage.at[which, slot], stage_sem.at[which, slot]
                )
            )
            staged[-1].start()
    for copy in staged:
        copy.wait()
    partners = n_head - 1 + jnp.where(is_last, 0, 1) + jnp.where(row_start, 0, 1)
    pl.semaphore_wait(barrier, partners)

    @pl.when(late)
    def _():
        pl.semaphore_signal(ready, inc=1, device_id=to_ctx(1), device_id_type=MESH)

    sends = []
    for slot in range(2):
        for d in (2, 1, 3):
            to = lax.rem(x + d, n_head)
            copy = pltpu.make_async_remote_copy(
                src_ref=stage.at[:, slot, :, pl.ds(at_block(to), HD)],
                dst_ref=kv_place(slot, x),
                send_sem=kv_send.at[slot, d],
                recv_sem=kv_recv.at[slot, x],
                device_id=(c, to),
                device_id_type=MESH,
            )
            copy.start()
            sends.append(copy)

    loads = []
    for slot in range(2):
        for i, (src, dst) in enumerate(((q_hbm, q_v), (do_hbm, do_v))):
            loads.append(
                pltpu.make_async_copy(src.at[slot], dst.at[slot], load_sem.at[i, slot])
            )
            loads[-1].start()
    for which in range(2):
        for slot in range(2):
            mine = stage[which, slot, :, pl.ds(at_block(x), HD)]
            kv[which, slot, pl.ds(at_block(x + 2), BLK), :] = mine

    acc[...] = jnp.zeros_like(acc)

    @pl.when(is_first)
    def _():
        kv[:, 0, 0:TAIL, :] = jnp.zeros((2, TAIL, HD), BF16)

    kk = lax.broadcasted_iota(jnp.int32, (BLK, HEADS * BLK), 0)
    qq = lax.broadcasted_iota(jnp.int32, (BLK, HEADS * BLK), 1) % BLK
    tri = jnp.where(kk <= qq, 0.0, -BIG).astype(F32)

    def wait_kv(slot, block):
        @pl.when(x != block)
        def _():
            place = kv_place(slot, block)
            pltpu.make_async_copy(place, place, kv_recv.at[slot, block]).wait()

    def relay(slot, step):
        return pltpu.make_async_remote_copy(
            src_ref=kv.at[:, slot, pl.ds(SPAN, TAIL), :],
            dst_ref=kv.at[:, slot, pl.ds(0, TAIL), :],
            send_sem=relay_send.at[slot],
            recv_sem=relay_recv.at[slot],
            device_id=to_ctx(step),
            device_id_type=MESH,
        )

    def tail_copy(slot, i, step):
        return pltpu.make_async_remote_copy(
            src_ref=tail_out.at[slot, i],
            dst_ref=tail_in.at[slot, i],
            send_sem=tail_send.at[slot, i],
            recv_sem=tail_recv.at[slot, i],
            device_id=to_ctx(step),
            device_id_type=MESH,
        )

    def has(slot):
        if isinstance(slot, int):
            return jnp.logical_not(is_first) if slot == 0 else jnp.logical_not(is_last)
        return jnp.where(slot == 0, c > 0, c < n_ctx - 1)

    def send_tail(slot, i):
        rows = pl.ds(i * BLK, BLK)
        tail_out[slot, i, 0] = (acc[0, slot, rows, :] * SCALE).astype(BF16)
        tail_out[slot, i, 1] = acc[1, slot, rows, :].astype(BF16)

        @pl.when(has(slot))
        def _():
            tail_copy(slot, i, 2 * slot - 1).start()

    def out_remote(slot, block):
        return pltpu.make_async_remote_copy(
            src_ref=out_v.at[slot, block],
            dst_ref=dkv_v.at[:, slot, :, pl.ds(at_block(x), HD)],
            send_sem=out_send.at[slot, block],
            recv_sem=out_recv.at[slot, x],
            device_id=(c, block),
            device_id_type=MESH,
        )

    def send_out(slot, block, extra=None):
        rows = pl.ds((block + 2) * BLK, BLK)
        for which in range(2):
            value = acc[which, slot, rows, :]
            if which == 0:
                value = value * SCALE
            if extra is not None:
                value = value + extra(which, block - 2)
            out_v[slot, block, which] = value.astype(BF16)

        @pl.when(x != block)
        def _():
            out_remote(slot, block).start()

        @pl.when(x == block)
        def _():
            place = dkv_v.at[:, slot, :, pl.ds(at_block(x), HD)]
            pltpu.make_async_copy(out_v.at[slot, block], place, out_recv.at[slot, x]).start()

    def span_of(slot):
        return jnp.where(slot == 0, c, 2 * n_ctx - 1 - c)

    tools = (q_v, do_v, dq_v, kv, acc, docs, tri)

    wait_kv(0, 3)
    wait_kv(0, 2)

    @pl.when(jnp.logical_not(is_last))
    def _():
        relay(0, 1).start()

    doc_copy.wait()
    loads[0].wait()
    loads[1].wait()
    wait_kv(0, 1)
    wait_kv(0, 0)
    block_grads(*tools, 0, span_of(0), 3, 4, 2)
    block_grads(*tools, 0, span_of(0), 2 - first, 3 - first, 2)

    @pl.when(early)
    def _():
        pl.semaphore_wait(ready, 1)

    wait_kv(1, 3)
    wait_kv(1, 2)

    @pl.when(jnp.logical_not(is_first))
    def _():
        relay(1, -1).start()

    wait_kv(1, 1)
    wait_kv(1, 0)

    @pl.when(is_last)
    def _():
        kv[:, 1, 0:TAIL, :] = kv[:, 0, SPAN : SPAN + TAIL, :]

    loads[2].wait()
    loads[3].wait()

    def front(slot):
        @pl.when(has(slot))
        def _():
            relay(slot, 1).wait_recv()

        swap = jnp.where(slot == 0, first, 0)
        block_grads(*tools, slot, span_of(slot), 0, 0, 3)
        block_grads(*tools, slot, span_of(slot), 1 + swap, 1 + swap, 3)
        send_tail(slot, 0)
        send_tail(slot, 1)

    front(lead)

    @pl.when(lead == 0)
    def _():
        send_out(0, 0)
        send_out(0, 1)

    @pl.when(lead == 1)
    def _():
        send_out(1, 0)

    front(1 - lead)

    @pl.when(lead == 1)
    def _():
        send_out(0, 0)
        send_out(0, 1)

    @pl.when(lead == 0)
    def _():
        send_out(1, 0)

    def tail_arrives(slot, i):
        @pl.when(has(1 - slot))
        def _():
            tail_copy(slot, i, 1).wait_recv()

    def extra_first(which, i):
        arrived = tail_in[0, i, which].astype(F32)
        mine = tail_out[1, i, which].astype(F32)
        return jnp.where(is_last, mine, arrived)

    def extra_second(which, i):
        return jnp.where(is_first, 0.0, tail_in[1, i, which].astype(F32))

    for i in range(2):
        tail_arrives(0, i)
        send_out(0, 2 + i, extra_first)

    @pl.when(is_first)
    def _():
        block_grads(*tools, 1, span_of(1), 2, 3, 2)
        block_grads(*tools, 1, span_of(1), 3, 3, 3)

    @pl.when(jnp.logical_not(is_first))
    def _():
        block_grads(*tools, 1, span_of(1), 2, 3, 2)
        block_grads(*tools, 1, span_of(1), 3, 4, 2)

    send_out(1, 1)

    for i in range(2):
        tail_arrives(1, i)
        send_out(1, 2 + i, extra_second)

    for copy in sends:
        copy.wait_send()
    for slot in range(2):

        @pl.when(has(1 - slot))
        def _():
            relay(slot, 1).wait_send()

        @pl.when(has(slot))
        def _():
            tail_copy(slot, 0, 1).wait_send()
            tail_copy(slot, 1, 1).wait_send()

        for block in range(4):

            @pl.when(x != block)
            def _():
                out_remote(slot, block).wait_send()

            place = dkv_v.at[:, slot, :, pl.ds(block * HD, HD)]
            pltpu.make_async_copy(place, place, out_recv.at[slot, block]).wait()


def store_kernel(dq_v, dkv_v, dq_hbm, dk_hbm, dv_hbm, sem):
    copies = []
    for slot in range(2):
        for block in range(4):
            rows = pl.ds(block * BLK, BLK)
            copies.append((dq_v.at[slot, rows, :], dq_hbm.at[slot, rows, :]))
    copies.append((dkv_v.at[0], dk_hbm))
    copies.append((dkv_v.at[1], dv_hbm))
    started = [
        pltpu.make_async_copy(src, dst, sem.at[i]) for i, (src, dst) in enumerate(copies)
    ]
    for copy in started:
        copy.start()
    for copy in started:
        copy.wait()


def per_device(n_ctx, n_head, query, key, value, d_out, doc_start):
    hbm = pl.BlockSpec(memory_space=pltpu.HBM)
    vmem = pl.BlockSpec(memory_space=pltpu.VMEM)
    dma = pltpu.SemaphoreType.DMA
    dq, dkv = pl.pallas_call(
        functools.partial(kernel, n_ctx, n_head),
        out_shape=(
            jax.ShapeDtypeStruct((2, SPAN, HEADS * HD), BF16),
            jax.ShapeDtypeStruct((2, 2, BLK, n_head * HD), BF16),
        ),
        in_specs=[hbm] * 5,
        out_specs=(vmem, vmem),
        scratch_shapes=[
            pltpu.VMEM((2, 2, BLK, n_head * HD), BF16),
            pltpu.VMEM((2, SPAN, HEADS * HD), BF16),
            pltpu.VMEM((2, SPAN, HEADS * HD), BF16),
            pltpu.VMEM((2, 2, EXT, HD), BF16),
            pltpu.VMEM((2, 2, EXT, HD), F32),
            pltpu.VMEM((2, 4, 2, BLK, HD), BF16),
            pltpu.VMEM((2, 2, 2, BLK, HD), BF16),
            pltpu.VMEM((2, 2, 2, BLK, HD), BF16),
            pltpu.SMEM(doc_start.shape, jnp.int32),
            dma((2, 2)),
            dma((2, 2)),
            dma,
            dma((2, 4)),
            dma((2, 4)),
            dma((2,)),
            dma((2,)),
            dma((2, 2)),
            dma((2, 2)),
            dma((2, 4)),
            dma((2, 4)),
            pltpu.SemaphoreType.REGULAR,
        ],
        compiler_params=pltpu.CompilerParams(
            collective_id=0, has_side_effects=True, vmem_limit_bytes=40 << 20
        ),
    )(*[
            pltpu.with_memory_space_constraint(a, pltpu.HBM)
            for a in (query[0], d_out[0], key[0], value[0], doc_start)
        ])
    d_query, d_key, d_value = pl.pallas_call(
        store_kernel,
        out_shape=(
            jax.ShapeDtypeStruct((2, SPAN, HEADS * HD), BF16),
            jax.ShapeDtypeStruct((2, BLK, n_head * HD), BF16),
            jax.ShapeDtypeStruct((2, BLK, n_head * HD), BF16),
        ),
        in_specs=[vmem, vmem],
        out_specs=(hbm, hbm, hbm),
        scratch_shapes=[dma((10,))],
        compiler_params=pltpu.CompilerParams(vmem_limit_bytes=1 << 20),
    )(dq, dkv)
    return d_query[None], d_key[None], d_value[None]


def solution(mesh):
    return jax.shard_map(
        functools.partial(per_device, mesh.shape["ctx"], mesh.shape["head"]),
        mesh=mesh,
        in_specs=(
            P("ctx", None, None, "head"),
            P("ctx", None, "head", None),
            P("ctx", None, "head", None),
            P("ctx", None, None, "head"),
            P(),
        ),
        out_specs=(
            P("ctx", None, None, "head"),
            P("ctx", None, "head", None),
            P("ctx", None, "head", None),
        ),
        check_vma=False,
    )
```
